512 devices in a mesh: clip: 4 (over x), tx: 16 (over z_lo, core), ty: 8 (over z_hi, y).
Axes of the slice: x: 4, y: 4, z: 16 (z_hi: 2, z_lo: 8; z = z_hi * 8 + z_lo), core: 2. Of those that a mesh axis runs over, the one named last changes fastest.
Arguments:
- query_states: bfloat16 [512, 128, 1152], P(('clip', 'tx', 'ty')), parts along dimension 0, may hold values from -64 to 64
- key_states: bfloat16 [512, 128, 1152], P(('clip', 'tx', 'ty')), parts along dimension 0, may hold values from -24 to 24
- value_states: bfloat16 [512, 128, 1152], P(('clip', 'tx', 'ty')), parts along dimension 0, may hold values from -6 to 6
- grad_output: bfloat16 [512, 128, 1152], P(('clip', 'tx', 'ty')), parts along dimension 0, may hold values from -6 to 6
- branch_gate: float32 [4608], P('clip'), parts along dimension 0, may hold values from 0.1 to 1.9
- out_weight: bfloat16 [1152, 1152], P('tx'), may hold values from -0.1875 to 0.1875
Outputs:
- query_grad: bfloat16 [512, 128, 1152], P(('clip', 'tx', 'ty')), parts along dimension 0
- key_grad: bfloat16 [512, 128, 1152], P(('clip', 'tx', 'ty')), parts along dimension 0
- value_grad: bfloat16 [512, 128, 1152], P(('clip', 'tx', 'ty')), parts along dimension 0
- gate_grad: float32 [4608], P('clip'), parts along dimension 0
The draws below stay inside these ranges and needn't reach their ends.
There are 4 independent parts, one for each index of `clip`. The reference program is written for one: setup_inputs(seed, part) draws one part's arguments, and reference() takes and returns one part's arrays. A program takes and returns all parts, laid end to end along the dimension named above; an argument that names none is the same for every part. Nothing has to cross between parts.
All inputs are finite; a program needn't handle non-finite values.
Results may differ from the reference program's by a relative error of at most 0.025.
Values may be sent and summed in bfloat16 or wider, within the bound.
No kernel may reach another device: no remote copies, remote signals or barrier semaphores. Data moves between devices by JAX's collectives and lax.ppermute only.
A program may use at most 64 MiB of HBM per device.

```python
import jax
import jax.numpy as jnp
from jax import lax

HEADS = 16
HEAD_DIM = 72
D = 1152
POS = 128
FRAMES = 128


def paired_draw(key):
    base = jax.random.fold_in(key, 4242)
    key_q, key_k = jax.random.split(base, 2)
    shape = (FRAMES, POS, D)
    queries = jnp.clip(jax.random.normal(key_q, shape, jnp.float32), -6.0, 6.0)
    keys_out = jnp.clip(jax.random.normal(key_k, shape, jnp.float32), -6.0, 6.0)
    return (queries, keys_out)


def draw_query_states(key, part):
    return paired_draw(key)[0].astype(jnp.bfloat16)


def draw_key_states(key, part):
    return paired_draw(key)[1].astype(jnp.bfloat16)


def steps_of(rng, dims, pieces, least, largest):
    gain = 1.0
    for axis_at, parts in pieces:
        steps = jax.random.uniform(jax.random.fold_in(jax.random.fold_in(rng, 6), axis_at), (parts,), jnp.float32, least / len(pieces), largest / len(pieces))
        gain = gain * jnp.repeat(jnp.exp(steps), dims[axis_at] // parts).reshape((-1,) + (1,) * (len(dims) - 1 - axis_at))
    return gain


def gaussian(stream_key, shape, deviation, reach, cuts=(), dtype=jnp.bfloat16):
    entries = jax.random.normal(stream_key, shape, jnp.float32) * deviation
    if len(cuts) > 0:
        entries = steps_of(stream_key, shape, cuts, -0.22, 0.18) * entries
    return jnp.clip(entries, min=-reach, max=reach).astype(dtype)


def setup_inputs(seed: int = 0, part: int = 0) -> dict:
    keys = jax.random.split(jax.random.key(seed), 7)
    own_keys = jax.random.split(jax.random.fold_in(keys[6], part), 7)
    return {
        "query_states": draw_query_states(jax.random.fold_in(jax.random.fold_in(keys[6], part), 71), part),
        "key_states": draw_key_states(jax.random.fold_in(jax.random.fold_in(keys[6], part), 71), part),
        "value_states": gaussian(own_keys[2], (FRAMES, POS, D), 1.0, 6.0, ((0, 128),)),
        "grad_output": gaussian(own_keys[3], (FRAMES, POS, D), 1.0, 6.0, ((0, 128),)),
        "branch_gate": jnp.clip(1.0 + 0.18 * jax.random.normal(own_keys[4], (D,), jnp.float32), 0.1, 1.9),
        "out_weight": gaussian(keys[5], (D, D), D ** -0.5, 0.1875, ((0, 16),)),
    }


def one_position(operands):
    queries, keys_in, values_in, grads_in = operands
    shape4 = (FRAMES, HEADS, HEAD_DIM)
    q_f = queries.reshape(shape4).astype(jnp.float32)
    k_f = keys_in.reshape(shape4).astype(jnp.float32)
    v_f = values_in.reshape(shape4).astype(jnp.float32)
    g_f = grads_in.reshape(shape4).astype(jnp.float32)
    factor = HEAD_DIM ** -0.5
    scores = jnp.einsum('fhd,ghd->hfg', q_f, k_f) * factor
    peak = jnp.max(scores, axis=-1, keepdims=True)
    expon = jnp.exp(scores - peak)
    probs = expon / jnp.sum(expon, axis=-1, keepdims=True)
    probs_b = probs.astype(jnp.bfloat16).astype(jnp.float32)
    attn_out = jnp.einsum('hfg,ghd->fhd', probs_b, v_f).astype(jnp.bfloat16)
    value_grad = jnp.einsum('hfg,fhd->ghd', probs_b, g_f).astype(jnp.bfloat16)
    dprobs = jnp.einsum('fhd,ghd->hfg', g_f, v_f)
    delta = jnp.sum(g_f * attn_out.astype(jnp.float32), axis=-1)
    delta = jnp.transpose(delta, (1, 0))[:, :, None]
    dscores = (probs * (dprobs - delta) * factor).astype(jnp.bfloat16).astype(jnp.float32)
    query_grad = jnp.einsum('hfg,ghd->fhd', dscores, k_f).astype(jnp.bfloat16)
    key_grad = jnp.einsum('hfg,fhd->ghd', dscores, q_f).astype(jnp.bfloat16)
    flat = (FRAMES, D)
    return (query_grad.reshape(flat), key_grad.reshape(flat), value_grad.reshape(flat), attn_out.reshape(flat))


def reference(query_states, key_states, value_states, grad_output, branch_gate, out_weight):
    gated = (grad_output.astype(jnp.float32) * branch_gate).astype(jnp.bfloat16)
    d_attn = jnp.dot(gated.reshape(FRAMES * POS, D), out_weight.T, preferred_element_type=jnp.float32)
    d_attn = d_attn.astype(jnp.bfloat16).reshape(FRAMES, POS, D)
    operands = tuple(jnp.transpose(arr, (1, 0, 2)) for arr in (query_states, key_states, value_states, d_attn))
    results = lax.map(one_position, operands)
    query_grad, key_grad, value_grad, attn_out = tuple(jnp.transpose(arr, (1, 0, 2)) for arr in results)
    branch_out = jnp.dot(attn_out.reshape(FRAMES * POS, D), out_weight, preferred_element_type=jnp.float32)
    gate_grad = jnp.sum(grad_output.reshape(FRAMES * POS, D).astype(jnp.float32) * branch_out, axis=0)
    return query_grad, key_grad, value_grad, gate_grad
```

```python
import functools

import jax
import jax.numpy as jnp
from jax import lax
from jax.experimental import pallas as pl
from jax.experimental.pallas import tpu as pltpu
from jax.sharding import Mesh
from jax.sharding import PartitionSpec as P

HEADS = 16
HEAD_DIM = 72
LANES = 128
WIDTH = HEADS * HEAD_DIM
TILES = WIDTH // LANES
AXES = ("clip", "zl", "core", "zh", "y")
GROUP = ("zl", "core", "zh", "y")
FACTOR = HEAD_DIM ** (-0.5)


def head_tiles(head):
    first = head * HEAD_DIM // LANES
    last = (head * HEAD_DIM + HEAD_DIM - 1) // LANES
    return first, last + 1


def attend_kernel(x_ref, w_ref, gate_ref, out_ref, gate_out_ref, da_ref):
    f32, bf16 = jnp.float32, jnp.bfloat16
    nt = (((1,), (1,)), ((), ()))
    nn = (((1,), (0,)), ((), ()))
    tn = (((0,), (0,)), ((), ()))
    frames = x_ref.shape[1]

    def cat(first, last):
        parts = [x_ref[t] for t in range(first, last)]
        return parts[0] if len(parts) == 1 else jnp.concatenate(parts, axis=1)

    go = cat(3 * TILES, 4 * TILES)
    gated = (go.astype(f32) * gate_ref[...]).astype(bf16)
    da_ref[...] = lax.dot_general(gated, w_ref[...], nt, preferred_element_type=f32).astype(bf16)

    acc = {}

    def add(kind, first, value):
        for n in range(value.shape[1] // LANES):
            key = (kind, first + n)
            part = value[:, n * LANES : (n + 1) * LANES]
            acc[key] = acc[key] + part if key in acc else part

    for head in range(HEADS):
        a, b = head_tiles(head)
        width = (b - a) * LANES
        lane = lax.broadcasted_iota(jnp.int32, (frames, width), 1) + a * LANES
        mask = (lane >= head * HEAD_DIM) & (lane < (head + 1) * HEAD_DIM)

        def masked(value):
            return jnp.where(mask, value, jnp.zeros_like(value))

        q = masked(cat(a, b))
        k = masked(cat(TILES + a, TILES + b))
        v = masked(cat(2 * TILES + a, 2 * TILES + b))
        g = masked(da_ref[:, a * LANES : b * LANES])
        scores = lax.dot_general(q, k, nt, preferred_element_type=f32) * FACTOR
        expon = jnp.exp(scores - jnp.max(scores, axis=-1, keepdims=True))
        probs = expon / jnp.sum(expon, axis=-1, keepdims=True)
        probs_b = probs.astype(bf16)
        add("o", a, lax.dot_general(probs_b, v, nn, preferred_element_type=f32))
        add("v", a, lax.dot_general(probs_b, g, tn, preferred_element_type=f32))
        dprobs = lax.dot_general(g, v, nt, preferred_element_type=f32)
        delta = jnp.sum(probs * dprobs, axis=-1, keepdims=True)
        dscores = (probs * (dprobs - delta) * FACTOR).astype(bf16)
        add("q", a, lax.dot_general(dscores, k, nn, preferred_element_type=f32))
        add("k", a, lax.dot_general(dscores, q, tn, preferred_element_type=f32))
    for n, kind in enumerate("qkv"):
        for t in range(TILES):
            out_ref[n * TILES + t] = acc[(kind, t)].astype(bf16)
    attn = jnp.concatenate([acc[("o", t)].astype(bf16) for t in range(TILES)], axis=1)
    branch = lax.dot_general(attn, w_ref[...], nn, preferred_element_type=f32)
    gate_out_ref[...] = jnp.sum(go.astype(f32) * branch, axis=0, keepdims=True)


def attend(x, weight, gate):
    frames = x.shape[1]
    vmem = pl.BlockSpec(memory_space=pltpu.VMEM)
    return pl.pallas_call(
        attend_kernel,
        out_shape=(
            jax.ShapeDtypeStruct((3 * TILES, frames, LANES), jnp.bfloat16),
            jax.ShapeDtypeStruct((1, WIDTH), jnp.float32),
        ),
        in_specs=[vmem, vmem, vmem],
        out_specs=(vmem, vmem),
        scratch_shapes=[pltpu.VMEM((frames, WIDTH), jnp.bfloat16)],
        compiler_params=pltpu.CompilerParams(vmem_limit_bytes=32 << 20),
        cost_estimate=pl.CostEstimate(
            flops=1_500_000_000, bytes_accessed=5_000_000, transcendentals=300_000
        ),
    )(x, weight, gate)


def z_spot(z):
    return (z % 8) * 2 + z // 8


def along_z(x, to):
    return lax.ppermute(x, ("zl", "zh"), [(z_spot(i), z_spot(to(i) % 16)) for i in range(16)])


def along(x, axis, shift, sources):
    return lax.ppermute(x, axis, [(i, (i + shift) % 4) for i in range(sources)])


def pick(stack, index):
    return lax.dynamic_index_in_dim(stack, index, 0, keepdims=False)


def gather_weight(shard):
    rows = 8
    z = lax.axis_index("zl")
    x = lax.axis_index("clip")
    y = lax.axis_index("y")
    core = lax.axis_index("core")
    row = jnp.minimum(x, 2) * 3 + jnp.minimum(y, 2)
    held = lax.dynamic_slice_in_dim(shard, row * rows, rows, 0)[None]
    held = jnp.concatenate([held, along_z(held, lambda i: i + 1)])
    held = jnp.concatenate([along_z(held, lambda i: i - 2), held])
    held = jnp.concatenate([held, along_z(held, lambda i: i + 4 if i % 2 == 0 else i - 4)])
    held = jnp.stack([pick(held, (z + 2 - n) % 8) for n in range(8)])
    parts = jnp.stack([held] + [along(held, "y", s, 3) for s in (1, 2, 3)])
    held = jnp.stack([pick(parts, (y - n) % 4) for n in range(3)])
    parts = jnp.stack([held] + [along(held, "clip", s, 3) for s in (1, 2, 3)])
    held = jnp.stack([pick(parts, (x - n) % 4) for n in range(3)])
    other = lax.ppermute(held, "core", [(0, 1), (1, 0)])
    both = jnp.stack([jnp.where(core == 0, held, other), jnp.where(core == 0, other, held)])
    return jnp.transpose(both, (3, 0, 1, 2, 4, 5)).reshape(WIDTH, WIDTH)


def sum_over_group(v):
    v = v + lax.ppermute(v, "core", [(0, 1), (1, 0)])
    v = v + along(v, "y", 1, 4) + along(v, "y", 2, 4) + along(v, "y", 3, 4)
    for step in (1, 4):
        hops = [along_z(v, lambda i, n=n: i + n * step) for n in (1, 2, 3)]
        v = v + hops[0] + hops[1] + hops[2]
    return v


def per_device(query_states, key_states, value_states, grad_output, branch_gate, out_weight):
    positions = grad_output.shape[1]
    sources = (query_states, key_states, value_states, grad_output)
    packed = jnp.concatenate([a.reshape(positions, TILES, LANES) for a in sources], axis=1)
    packed = packed.reshape(positions, TILES, 4, LANES)
    moved = lax.all_to_all(packed, GROUP, split_axis=0, concat_axis=0, tiled=True)
    frames = moved.shape[0]
    moved = jnp.transpose(moved.reshape(frames, 4 * TILES, LANES), (1, 0, 2))
    weight = gather_weight(out_weight)
    grads, terms = attend(moved, weight, branch_gate.reshape(1, WIDTH))
    outgoing = jnp.transpose(grads, (1, 0, 2))
    outgoing = jnp.pad(outgoing, ((0, 0), (0, 1), (0, 0))).reshape(frames, 7, 4, LANES)
    returned = lax.all_to_all(outgoing, GROUP, split_axis=0, concat_axis=0, tiled=True)
    returned = returned.reshape(positions, 28, LANES)
    outs = tuple(
        returned[:, n * TILES : (n + 1) * TILES].reshape(1, positions, WIDTH) for n in range(3)
    )
    return outs + (sum_over_group(terms).reshape(WIDTH),)


def solution(mesh):
    split = Mesh(mesh.devices.reshape(mesh.shape["clip"], 8, 2, 2, 4), AXES)
    rows = P(AXES, None, None)
    return jax.shard_map(
        per_device,
        mesh=split,
        in_specs=(rows, rows, rows, rows, P("clip"), P(("zl", "core"), None)),
        out_specs=(rows, rows, rows, P("clip")),
        check_vma=False,
    )
```

```python
import functools

import jax
import jax.numpy as jnp
from jax import lax
from jax.experimental import pallas as pl
from jax.experimental.pallas import tpu as pltpu
from jax.sharding import Mesh
from jax.sharding import PartitionSpec as P

HEADS = 16
HEAD_DIM = 72
LANES = 128
WIDTH = HEADS * HEAD_DIM
TILES = WIDTH // LANES
AXES = ("clip", "zl", "core", "zh", "y")
GROUP = ("zl", "core", "zh", "y")
GATE_ROWS = 5
ROWS_OUT = 3 * TILES + GATE_ROWS
FACTOR = HEAD_DIM ** (-0.5)


def head_tiles(head):
    first = head * HEAD_DIM // LANES
    last = (head * HEAD_DIM + HEAD_DIM - 1) // LANES
    return first, last + 1


def attend_kernel(moved_ref, w_ref, gate_ref, out_ref, x_ref, da_ref):
    f32, bf16 = jnp.float32, jnp.bfloat16
    nt = (((1,), (1,)), ((), ()))
    nn = (((1,), (0,)), ((), ()))
    tn = (((0,), (0,)), ((), ()))
    frames = moved_ref.shape[0]
    x_ref[...] = jnp.transpose(moved_ref[...].reshape(frames, 4 * TILES, LANES), (1, 0, 2))

    def cat(first, last):
        parts = [x_ref[t] for t in range(first, last)]
        return parts[0] if len(parts) == 1 else jnp.concatenate(parts, axis=1)

    go = cat(3 * TILES, 4 * TILES)
    gated = (go.astype(f32) * gate_ref[...]).astype(bf16)
    da_ref[...] = lax.dot_general(gated, w_ref[...], nt, preferred_element_type=f32).astype(bf16)

    acc = {}

    def add(kind, first, value):
        for n in range(value.shape[1] // LANES):
            key = (kind, first + n)
            part = value[:, n * LANES : (n + 1) * LANES]
            acc[key] = acc[key] + part if key in acc else part

    def operands(head):
        a, b = head_tiles(head)
        lane = lax.broadcasted_iota(jnp.int32, (frames, (b - a) * LANES), 1) + a * LANES
        mask = (lane >= head * HEAD_DIM) & (lane < (head + 1) * HEAD_DIM)

        def masked(value):
            return jnp.where(mask, value, jnp.zeros_like(value))

        q = masked(cat(a, b))
        k = masked(cat(TILES + a, TILES + b))
        v = masked(cat(2 * TILES + a, 2 * TILES + b))
        g = masked(da_ref[:, a * LANES : b * LANES])
        return a, q, k, v, g

    for first in range(0, HEADS, 8):
        heads = range(first, first + 8)
        ops = [operands(h) for h in heads]
        scores = [lax.dot_general(q, k, nt, preferred_element_type=f32) for _, q, k, v, g in ops]
        dprobs = [lax.dot_general(g, v, nt, preferred_element_type=f32) for _, q, k, v, g in ops]
        scores = [s * FACTOR for s in scores]
        expon = [jnp.exp(s - jnp.max(s, axis=-1, keepdims=True)) for s in scores]
        probs = [e / jnp.sum(e, axis=-1, keepdims=True) for e in expon]
        probs_b = [p.astype(bf16) for p in probs]
        delta = [jnp.sum(p * d, axis=-1, keepdims=True) for p, d in zip(probs, dprobs)]
        dscores = [
            (p * (d - e) * FACTOR).astype(bf16) for p, d, e in zip(probs, dprobs, delta)
        ]
        for (a, q, k, v, g), p, d in zip(ops, probs_b, dscores):
            add("o", a, lax.dot_general(p, v, nn, preferred_element_type=f32))
            add("v", a, lax.dot_general(p, g, tn, preferred_element_type=f32))
            add("q", a, lax.dot_general(d, k, nn, preferred_element_type=f32))
            add("k", a, lax.dot_general(d, q, tn, preferred_element_type=f32))
    attn = jnp.concatenate([acc[("o", t)].astype(bf16) for t in range(TILES)], axis=1)
    branch = lax.dot_general(attn, w_ref[...], nn, preferred_element_type=f32)
    terms = jnp.sum(go.astype(f32) * branch, axis=0, keepdims=True)
    rows = [terms[:, t * LANES : (t + 1) * LANES] for t in range(TILES)]

    out = [acc[(kind, t)].astype(bf16) for kind in "qkv" for t in range(TILES)]
    for n in range(GATE_ROWS):
        pair = [jnp.broadcast_to(rows[m], (8, LANES)) for m in (n, n + GATE_ROWS - 1)]
        block = jnp.concatenate(pair, axis=0).astype(bf16)
        out.append(jnp.concatenate([block] * (frames // 16), axis=0))
    out_ref[...] = jnp.transpose(jnp.stack(out), (1, 0, 2)).reshape(out_ref.shape)


def attend(x, weight, gate):
    frames = x.shape[0]
    vmem = pl.BlockSpec(memory_space=pltpu.VMEM)
    return pl.pallas_call(
        attend_kernel,
        out_shape=jax.ShapeDtypeStruct((frames, ROWS_OUT // 4, 4, LANES), jnp.bfloat16),
        in_specs=[vmem, vmem, vmem],
        out_specs=vmem,
        scratch_shapes=[
            pltpu.VMEM((4 * TILES, frames, LANES), jnp.bfloat16),
            pltpu.VMEM((frames, WIDTH), jnp.bfloat16),
        ],
        compiler_params=pltpu.CompilerParams(vmem_limit_bytes=12 << 20),
        cost_estimate=pl.CostEstimate(
            flops=1_500_000_000, bytes_accessed=5_000_000, transcendentals=300_000
        ),
    )(x, weight, gate)


def pack_kernel(*refs):
    out_ref = refs[-1]
    tiles = [ref[0, :, t * LANES : (t + 1) * LANES] for ref in refs[:-1] for t in range(TILES)]
    out_ref[...] = jnp.transpose(jnp.stack(tiles), (1, 0, 2)).reshape(out_ref.shape)


def pack(arrays):
    positions = arrays[0].shape[1]
    vmem = pl.BlockSpec(memory_space=pltpu.VMEM)
    shape = (positions, len(arrays) * TILES // 4, 4, LANES)
    return pl.pallas_call(
        pack_kernel,
        out_shape=jax.ShapeDtypeStruct(shape, jnp.bfloat16),
        in_specs=[vmem] * len(arrays),
        out_specs=vmem,
        cost_estimate=pl.CostEstimate(flops=0, bytes_accessed=2_400_000, transcendentals=0),
    )(*arrays)


def unpack_kernel(x_ref, *out_refs):
    positions, quads = x_ref.shape[0], x_ref.shape[1]
    tiles = jnp.transpose(x_ref[...].reshape(positions, quads * 4, LANES), (1, 0, 2))
    for n, ref in enumerate(out_refs):
        for t in range(TILES):
            ref[0, :, t * LANES : (t + 1) * LANES] = tiles[n * TILES + t]


def unpack(x, count):
    positions = x.shape[0]
    vmem = pl.BlockSpec(memory_space=pltpu.VMEM)
    return pl.pallas_call(
        unpack_kernel,
        out_shape=(jax.ShapeDtypeStruct((1, positions, WIDTH), jnp.bfloat16),) * count,
        in_specs=[vmem],
        out_specs=(vmem,) * count,
        cost_estimate=pl.CostEstimate(flops=0, bytes_accessed=1_800_000, transcendentals=0),
    )(x)


def along(x, axis, shift):
    return lax.ppermute(x, axis, [(i, (i + shift) % 4) for i in range(4)])


def fetch_pairs():
    def spot(x, z, y):
        return ((x * 8 + z % 8) * 2 + z // 8) * 4 + y

    pairs = []
    for x in range(4):
        for y in range(4):
            far = (4 * x + y) // 2 - 3
            pairs += [(spot(x, (z + far) % 16, y), spot(x, z, y)) for z in range(16)]
    return pairs


PART = 40


def assemble_kernel(at_ref, own_ref, other_ref, out_ref):
    x, y, z, core = [at_ref[n] for n in range(4)]
    rows = out_ref.shape[2]

    def copy(source, slot):
        for n in range(8):
            first = lax.rem(n - z + 11, 8) * 2
            for half in range(2):
                owner = first + half
                s = lax.rem(x - lax.div(owner, 4) + 4, 4)
                t = lax.rem(y - lax.rem(owner, 4) + 4, 4)
                if half == 0:
                    out_ref[n, slot, :PART] = source[s, t]
                else:
                    out_ref[n, slot, PART:] = source[s, t, 2 * PART - rows :]

    @pl.when(core == 0)
    def _():
        copy(own_ref, 0)
        copy(other_ref, 1)

    @pl.when(core != 0)
    def _():
        copy(other_ref, 0)
        copy(own_ref, 1)


def assemble(at, own, other, rows):
    vmem = pl.BlockSpec(memory_space=pltpu.VMEM)
    return pl.pallas_call(
        assemble_kernel,
        out_shape=jax.ShapeDtypeStruct((8, 2, rows, WIDTH), jnp.bfloat16),
        in_specs=[pl.BlockSpec(memory_space=pltpu.SMEM), vmem, vmem],
        out_specs=vmem,
        compiler_params=pltpu.CompilerParams(vmem_limit_bytes=10 << 20),
        cost_estimate=pl.CostEstimate(flops=0, bytes_accessed=1000, transcendentals=0),
    )(at, own, other)


def gather_weight(shard, later):
    rows = shard.shape[0]
    y = lax.axis_index("y")
    held = jnp.where(y % 2 == 0, shard[:PART], shard[rows - PART :])
    held = lax.ppermute(held, ("clip", "zl", "zh", "y"), fetch_pairs())
    held, later = lax.optimization_barrier((held, later))
    held = jnp.stack([held] + [along(held, "y", s) for s in (1, 2, 3)])
    held = jnp.stack([held] + [along(held, "clip", s) for s in (1, 2, 3)])
    other = lax.ppermute(held, "core", [(0, 1), (1, 0)])
    at = jnp.stack([lax.axis_index(n) for n in ("clip", "y", "zl", "core")]).astype(jnp.int32)
    return assemble(at, held, other, rows).reshape(WIDTH, WIDTH), later


def sum_of_terms(pieces):
    own = jnp.sum(pieces.astype(jnp.float32), axis=0)
    other = lax.ppermute(own, "core", [(0, 1), (1, 0)])
    core = lax.axis_index("core")
    low = jnp.where(core == 0, own, other)
    high = jnp.where(core == 0, other, own)
    return jnp.concatenate([low, high[1:]], axis=0).reshape(WIDTH)


def per_device(query_states, key_states, value_states, grad_output, branch_gate, out_weight):
    packed = pack((query_states, key_states, value_states, grad_output))
    weight, packed = gather_weight(out_weight, packed)
    moved = lax.all_to_all(packed, GROUP, split_axis=0, concat_axis=0, tiled=True)
    grads = attend(moved, weight, branch_gate.reshape(1, WIDTH))
    returned = lax.all_to_all(grads, GROUP, split_axis=0, concat_axis=0, tiled=True)
    sent = returned.reshape(returned.shape[0], ROWS_OUT, LANES)
    gate_grad = sum_of_terms(sent[:, 3 * TILES :])
    return tuple(unpack(returned, 3)) + (gate_grad,)


def solution(mesh):
    split = Mesh(mesh.devices.reshape(mesh.shape["clip"], 8, 2, 2, 4), AXES)
    rows = P(AXES, None, None)
    return jax.shard_map(
        per_device,
        mesh=split,
        in_specs=(rows, rows, rows, rows, P("clip"), P(("zl", "core"), None)),
        out_specs=(rows, rows, rows, P("clip")),
        check_vma=False,
    )
```

```python
import functools

import jax
import jax.numpy as jnp
from jax import lax
from jax.experimental import pallas as pl
from jax.experimental.pallas import tpu as pltpu
from jax.sharding import Mesh
from jax.sharding import PartitionSpec as P

HEADS = 16
HEAD_DIM = 72
LANES = 128
WIDTH = HEADS * HEAD_DIM
TILES = WIDTH // LANES
AXES = ("clip", "zl", "core", "zh", "y")
GROUP = ("zl", "core", "zh", "y")
GATE_ROWS = 5
ROWS_OUT = 3 * TILES + GATE_ROWS
FACTOR = HEAD_DIM ** (-0.5)


def head_tiles(head):
    first = head * HEAD_DIM // LANES
    last = (head * HEAD_DIM + HEAD_DIM - 1) // LANES
    return first, last + 1


def attend_kernel(moved_ref, w_ref, gate_ref, out_ref, x_ref, da_ref):
    f32, bf16 = jnp.float32, jnp.bfloat16
    nt = (((1,), (1,)), ((), ()))
    nn = (((1,), (0,)), ((), ()))
    tn = (((0,), (0,)), ((), ()))
    frames = moved_ref.shape[0]
    x_ref[...] = jnp.transpose(moved_ref[...].reshape(frames, 4 * TILES, LANES), (1, 0, 2))

    def cat(first, last):
        parts = [x_ref[t] for t in range(first, last)]
        return parts[0] if len(parts) == 1 else jnp.concatenate(parts, axis=1)

    go = cat(3 * TILES, 4 * TILES)
    gated = (go.astype(f32) * gate_ref[...]).astype(bf16)
    da_ref[...] = lax.dot_general(gated, w_ref[...], nt, preferred_element_type=f32).astype(bf16)

    acc = {}

    def add(kind, first, value):
        for n in range(2):
            key = (kind, first + n)
            part = value[:, n * LANES : (n + 1) * LANES]
            acc[key] = acc[key] + part if key in acc else part

    lane = lax.broadcasted_iota(jnp.int32, (frames, 2 * LANES), 1)

    def both_heads(value, start):
        zero = jnp.zeros_like(value)
        heads = [
            jnp.where((lane >= at) & (lane < at + HEAD_DIM), value, zero)
            for at in (start, start + HEAD_DIM)
        ]
        return jnp.concatenate(heads, axis=0)

    def operands(pair):
        tile, start = divmod(2 * pair * HEAD_DIM, LANES)
        q, k, v = [cat(n * TILES + tile, n * TILES + tile + 2) for n in range(3)]
        g = da_ref[:, tile * LANES : (tile + 2) * LANES]
        return (tile, q, g) + tuple(both_heads(value, start) for value in (q, k, v, g))

    def heads_of(value):
        return value[:, :frames], value[:, frames:]

    for first in range(0, HEADS // 2, 4):
        ops = [operands(pair) for pair in range(first, first + 4)]
        scores = [lax.dot_general(o[1], o[4], nt, preferred_element_type=f32) for o in ops]
        dprobs = [lax.dot_general(o[2], o[5], nt, preferred_element_type=f32) for o in ops]
        scores = [s * FACTOR for pair in scores for s in heads_of(pair)]
        dprobs = [d for pair in dprobs for d in heads_of(pair)]
        expon = [jnp.exp(s - jnp.max(s, axis=-1, keepdims=True)) for s in scores]
        probs = [e / jnp.sum(e, axis=-1, keepdims=True) for e in expon]
        delta = [jnp.sum(p * d, axis=-1, keepdims=True) for p, d in zip(probs, dprobs)]
        dscores = [
            (p * (d - e) * FACTOR).astype(bf16) for p, d, e in zip(probs, dprobs, delta)
        ]
        probs = [p.astype(bf16) for p in probs]
        for n, (tile, _, _, q, k, v, g) in enumerate(ops):
            p, d = probs[2 * n : 2 * n + 2], dscores[2 * n : 2 * n + 2]
            p_wide, d_wide = jnp.concatenate(p, axis=1), jnp.concatenate(d, axis=1)
            p_tall, d_tall = jnp.concatenate(p, axis=0), jnp.concatenate(d, axis=0)
            add("o", tile, lax.dot_general(p_wide, v, nn, preferred_element_type=f32))
            add("v", tile, lax.dot_general(p_tall, g, tn, preferred_element_type=f32))
            add("q", tile, lax.dot_general(d_wide, k, nn, preferred_element_type=f32))
            add("k", tile, lax.dot_general(d_tall, q, tn, preferred_element_type=f32))
    attn = jnp.concatenate([acc[("o", t)].astype(bf16) for t in range(TILES)], axis=1)
    branch = lax.dot_general(attn, w_ref[...], nn, preferred_element_type=f32)
    terms = jnp.sum(go.astype(f32) * branch, axis=0, keepdims=True)
    rows = [terms[:, t * LANES : (t + 1) * LANES] for t in range(TILES)]

    out = [acc[(kind, t)].astype(bf16) for kind in "qkv" for t in range(TILES)]
    for n in range(GATE_ROWS):
        pair = [jnp.broadcast_to(rows[m], (8, LANES)) for m in (n, n + GATE_ROWS - 1)]
        block = jnp.concatenate(pair, axis=0).astype(bf16)
        out.append(jnp.concatenate([block] * (frames // 16), axis=0))
    out_ref[...] = jnp.transpose(jnp.stack(out), (1, 0, 2)).reshape(out_ref.shape)


def attend(x, weight, gate):
    frames = x.shape[0]
    vmem = pl.BlockSpec(memory_space=pltpu.VMEM)
    return pl.pallas_call(
        attend_kernel,
        out_shape=jax.ShapeDtypeStruct((frames, ROWS_OUT // 4, 4, LANES), jnp.bfloat16),
        in_specs=[vmem, vmem, vmem],
        out_specs=vmem,
        scratch_shapes=[
            pltpu.VMEM((4 * TILES, frames, LANES), jnp.bfloat16),
            pltpu.VMEM((frames, WIDTH), jnp.bfloat16),
        ],
        compiler_params=pltpu.CompilerParams(vmem_limit_bytes=12 << 20),
        cost_estimate=pl.CostEstimate(
            flops=1_500_000_000, bytes_accessed=5_000_000, transcendentals=300_000
        ),
    )(x, weight, gate)


def pack_kernel(*refs):
    out_ref = refs[-1]
    tiles = [ref[0, :, t * LANES : (t + 1) * LANES] for ref in refs[:-1] for t in range(TILES)]
    out_ref[...] = jnp.transpose(jnp.stack(tiles), (1, 0, 2)).reshape(out_ref.shape)


def pack(arrays):
    positions = arrays[0].shape[1]
    step = positions // 2
    shape = (positions, len(arrays) * TILES // 4, 4, LANES)
    return pl.pallas_call(
        pack_kernel,
        out_shape=jax.ShapeDtypeStruct(shape, jnp.bfloat16),
        grid=(2,),
        in_specs=[pl.BlockSpec((1, step, WIDTH), lambda i: (0, i, 0))] * len(arrays),
        out_specs=pl.BlockSpec((step,) + shape[1:], lambda i: (i, 0, 0, 0)),
        cost_estimate=pl.CostEstimate(flops=0, bytes_accessed=2_400_000, transcendentals=0),
    )(*arrays)


def unpack_kernel(x_ref, *out_refs):
    positions, quads = x_ref.shape[0], x_ref.shape[1]
    tiles = jnp.transpose(x_ref[...].reshape(positions, quads * 4, LANES), (1, 0, 2))
    for n, ref in enumerate(out_refs):
        for t in range(TILES):
            ref[0, :, t * LANES : (t + 1) * LANES] = tiles[n * TILES + t]


def unpack(x, count):
    positions = x.shape[0]
    step = positions // 2
    return pl.pallas_call(
        unpack_kernel,
        out_shape=(jax.ShapeDtypeStruct((1, positions, WIDTH), jnp.bfloat16),) * count,
        grid=(2,),
        in_specs=[pl.BlockSpec((step,) + x.shape[1:], lambda i: (i, 0, 0, 0))],
        out_specs=(pl.BlockSpec((1, step, WIDTH), lambda i: (0, i, 0)),) * count,
        cost_estimate=pl.CostEstimate(flops=0, bytes_accessed=1_800_000, transcendentals=0),
    )(x)


def along(x, axis, shift):
    return lax.ppermute(x, axis, [(i, (i + shift) % 4) for i in range(4)])


def fetch_pairs():
    def spot(x, z, y):
        return ((x * 8 + z % 8) * 2 + z // 8) * 4 + y

    pairs = []
    for x in range(4):
        for y in range(4):
            far = (4 * x + y) // 2 - 3
            pairs += [(spot(x, (z + far) % 16, y), spot(x, z, y)) for z in range(16)]
    return pairs


PART = 40


def assemble_kernel(at_ref, own_ref, other_ref, out_ref):
    x, y, z = [at_ref[n] for n in range(3)]
    rows = out_ref.shape[2]

    def copy(source, slot):
        for n in range(8):
            first = lax.rem(n - z + 11, 8) * 2
            for half in range(2):
                owner = first + half
                s = lax.rem(x - lax.div(owner, 4) + 4, 4)
                t = lax.rem(y - lax.rem(owner, 4) + 4, 4)
                if half == 0:
                    out_ref[n, slot, :PART] = source[s, t]
                else:
                    out_ref[n, slot, PART:] = source[s, t, 2 * PART - rows :]

    copy(own_ref, 0)
    copy(other_ref, 1)


def assemble(at, own, other, rows):
    vmem = pl.BlockSpec(memory_space=pltpu.VMEM)
    return pl.pallas_call(
        assemble_kernel,
        out_shape=jax.ShapeDtypeStruct((8, 2, rows, WIDTH), jnp.bfloat16),
        in_specs=[pl.BlockSpec(memory_space=pltpu.SMEM), vmem, vmem],
        out_specs=vmem,
        compiler_params=pltpu.CompilerParams(vmem_limit_bytes=10 << 20),
        cost_estimate=pl.CostEstimate(flops=0, bytes_accessed=1000, transcendentals=0),
    )(at, own, other)


def gather_weight(shard, later):
    rows = shard.shape[0]
    y = lax.axis_index("y")
    held = lax.ppermute(shard, ("clip", "zl", "zh", "y"), fetch_pairs())
    held, later = lax.optimization_barrier((held, later))
    held = jnp.where(y % 2 == 0, held[:PART], held[rows - PART :])
    held = jnp.stack([held] + [along(held, "y", s) for s in (1, 2, 3)])
    held = jnp.stack([held] + [along(held, "clip", s) for s in (1, 2, 3)])
    other = lax.ppermute(held, "core", [(0, 1), (1, 0)])
    at = jnp.stack([lax.axis_index(n) for n in ("clip", "y", "zl")]).astype(jnp.int32)
    pairs = assemble(at, held, other, rows)
    even = lax.axis_index("core") == 0
    pairs = jnp.where(even, pairs, pairs[:, ::-1])
    return pairs.reshape(WIDTH, WIDTH), later


def sum_of_terms(pieces):
    own = jnp.sum(pieces.astype(jnp.float32), axis=0)
    other = lax.ppermute(own, "core", [(0, 1), (1, 0)])
    core = lax.axis_index("core")
    low = jnp.where(core == 0, own, other)
    high = jnp.where(core == 0, other, own)
    return jnp.concatenate([low, high[1:]], axis=0).reshape(WIDTH)


def per_device(query_states, key_states, value_states, grad_output, branch_gate, out_weight):
    packed = pack((query_states, key_states, value_states, grad_output))
    weight, packed = gather_weight(out_weight, packed)
    moved = lax.all_to_all(packed, GROUP, split_axis=0, concat_axis=0, tiled=True)
    grads = attend(moved, weight, branch_gate.reshape(1, WIDTH))
    returned = lax.all_to_all(grads, GROUP, split_axis=0, concat_axis=0, tiled=True)
    sent = returned.reshape(returned.shape[0], ROWS_OUT, LANES)
    gate_grad = sum_of_terms(sent[:, 3 * TILES :])
    return tuple(unpack(returned, 3)) + (gate_grad,)


def solution(mesh):
    split = Mesh(mesh.devices.reshape(mesh.shape["clip"], 8, 2, 2, 4), AXES)
    rows = P(AXES, None, None)
    return jax.shard_map(
        per_device,
        mesh=split,
        in_specs=(rows, rows, rows, rows, P("clip"), P(("zl", "core"), None)),
        out_specs=(rows, rows, rows, P("clip")),
        check_vma=False,
    )
```

```python
import functools

import jax
import jax.numpy as jnp
from jax import lax
from jax.experimental import pallas as pl
from jax.experimental.pallas import tpu as pltpu
from jax.sharding import Mesh
from jax.sharding import PartitionSpec as P

HEADS = 16
HEAD_DIM = 72
LANES = 128
WIDTH = HEADS * HEAD_DIM
TILES = WIDTH // LANES
AXES = ("clip", "zl", "core", "zh", "y")
GROUP = ("zl", "core", "zh", "y")
GATE_ROWS = 5
ROWS_OUT = 3 * TILES + GATE_ROWS
FACTOR = HEAD_DIM ** (-0.5)


def head_tiles(head):
    first = head * HEAD_DIM // LANES
    last = (head * HEAD_DIM + HEAD_DIM - 1) // LANES
    return first, last + 1


def attend_kernel(moved_ref, w_ref, gate_ref, out_ref, x_ref, da_ref):
    f32, bf16 = jnp.float32, jnp.bfloat16
    nt = (((1,), (1,)), ((), ()))
    nn = (((1,), (0,)), ((), ()))
    tn = (((0,), (0,)), ((), ()))
    frames = moved_ref.shape[0]
    x_ref[...] = jnp.transpose(moved_ref[...].reshape(frames, 4 * TILES, LANES), (1, 0, 2))

    def cat(first, last):
        parts = [x_ref[t] for t in range(first, last)]
        return parts[0] if len(parts) == 1 else jnp.concatenate(parts, axis=1)

    go = cat(3 * TILES, 4 * TILES)
    gated = (go.astype(f32) * gate_ref[...]).astype(bf16)
    da_ref[...] = lax.dot_general(gated, w_ref[...], nt, preferred_element_type=f32).astype(bf16)

    acc = {}

    def add(kind, first, value):
        for n in range(2):
            key = (kind, first + n)
            part = value[:, n * LANES : (n + 1) * LANES]
            acc[key] = acc[key] + part if key in acc else part

    lane = lax.broadcasted_iota(jnp.int32, (frames, 2 * LANES), 1)

    def both_heads(value, start):
        zero = jnp.zeros_like(value)
        heads = [
            jnp.where((lane >= at) & (lane < at + HEAD_DIM), value, zero)
            for at in (start, start + HEAD_DIM)
        ]
        return jnp.concatenate(heads, axis=0)

    def operands(pair):
        tile, start = divmod(2 * pair * HEAD_DIM, LANES)
        q, k, v = [cat(n * TILES + tile, n * TILES + tile + 2) for n in range(3)]
        g = da_ref[:, tile * LANES : (tile + 2) * LANES]
        return (tile, q, g) + tuple(both_heads(value, start) for value in (q, k, v, g))

    def heads_of(value):
        return value[:, :frames], value[:, frames:]

    for first in range(0, HEADS // 2, 4):
        ops = [operands(pair) for pair in range(first, first + 4)]
        scores = [lax.dot_general(o[1], o[4], nt, preferred_element_type=f32) for o in ops]
        dprobs = [lax.dot_general(o[2], o[5], nt, preferred_element_type=f32) for o in ops]
        scores = [s * FACTOR for pair in scores for s in heads_of(pair)]
        dprobs = [d for pair in dprobs for d in heads_of(pair)]
        expon = [jnp.exp(s - jnp.max(s, axis=-1, keepdims=True)) for s in scores]
        probs = [e / jnp.sum(e, axis=-1, keepdims=True) for e in expon]
        delta = [jnp.sum(p * d, axis=-1, keepdims=True) for p, d in zip(probs, dprobs)]
        dscores = [
            (p * (d - e) * FACTOR).astype(bf16) for p, d, e in zip(probs, dprobs, delta)
        ]
        probs = [p.astype(bf16) for p in probs]
        for n, (tile, _, _, q, k, v, g) in enumerate(ops):
            p, d = probs[2 * n : 2 * n + 2], dscores[2 * n : 2 * n + 2]
            p_wide, d_wide = jnp.concatenate(p, axis=1), jnp.concatenate(d, axis=1)
            p_tall, d_tall = jnp.concatenate(p, axis=0), jnp.concatenate(d, axis=0)
            add("o", tile, lax.dot_general(p_wide, v, nn, preferred_element_type=f32))
            add("v", tile, lax.dot_general(p_tall, g, tn, preferred_element_type=f32))
            add("q", tile, lax.dot_general(d_wide, k, nn, preferred_element_type=f32))
            add("k", tile, lax.dot_general(d_tall, q, tn, preferred_element_type=f32))
    attn = jnp.concatenate([acc[("o", t)].astype(bf16) for t in range(TILES)], axis=1)
    branch = lax.dot_general(attn, w_ref[...], nn, preferred_element_type=f32)
    terms = jnp.sum(go.astype(f32) * branch, axis=0, keepdims=True)
    rows = [terms[:, t * LANES : (t + 1) * LANES] for t in range(TILES)]

    out = [acc[(kind, t)].astype(bf16) for kind in "qkv" for t in range(TILES)]
    for n in range(GATE_ROWS):
        pair = [jnp.broadcast_to(rows[m], (8, LANES)) for m in (n, n + GATE_ROWS - 1)]
        block = jnp.concatenate(pair, axis=0).astype(bf16)
        out.append(jnp.concatenate([block] * (frames // 16), axis=0))
    out_ref[...] = jnp.transpose(jnp.stack(out), (1, 0, 2)).reshape(out_ref.shape)


def attend(x, weight, gate):
    frames = x.shape[0]
    vmem = pl.BlockSpec(memory_space=pltpu.VMEM)
    return pl.pallas_call(
        attend_kernel,
        out_shape=jax.ShapeDtypeStruct((frames, ROWS_OUT // 4, 4, LANES), jnp.bfloat16),
        in_specs=[vmem, vmem, vmem],
        out_specs=vmem,
        scratch_shapes=[
            pltpu.VMEM((4 * TILES, frames, LANES), jnp.bfloat16),
            pltpu.VMEM((frames, WIDTH), jnp.bfloat16),
        ],
        compiler_params=pltpu.CompilerParams(vmem_limit_bytes=12 << 20),
        cost_estimate=pl.CostEstimate(
            flops=1_500_000_000, bytes_accessed=5_000_000, transcendentals=300_000
        ),
    )(x, weight, gate)


def pack_kernel(*refs):
    out_ref = refs[-1]
    tiles = [ref[0, :, t * LANES : (t + 1) * LANES] for ref in refs[:-1] for t in range(TILES)]
    out_ref[...] = jnp.transpose(jnp.stack(tiles), (1, 0, 2)).reshape(out_ref.shape)


def pack(arrays):
    positions = arrays[0].shape[1]
    step = positions // 2
    shape = (positions, len(arrays) * TILES // 4, 4, LANES)
    return pl.pallas_call(
        pack_kernel,
        out_shape=jax.ShapeDtypeStruct(shape, jnp.bfloat16),
        grid=(2,),
        in_specs=[pl.BlockSpec((1, step, WIDTH), lambda i: (0, i, 0))] * len(arrays),
        out_specs=pl.BlockSpec((step,) + shape[1:], lambda i: (i, 0, 0, 0)),
        cost_estimate=pl.CostEstimate(flops=0, bytes_accessed=2_400_000, transcendentals=0),
    )(*arrays)


def unpack_kernel(x_ref, *out_refs):
    positions, quads = x_ref.shape[0], x_ref.shape[1]
    tiles = jnp.transpose(x_ref[...].reshape(positions, quads * 4, LANES), (1, 0, 2))
    for n, ref in enumerate(out_refs):
        for t in range(TILES):
            ref[0, :, t * LANES : (t + 1) * LANES] = tiles[n * TILES + t]


def unpack(x, count):
    positions = x.shape[0]
    step = positions // 2
    return pl.pallas_call(
        unpack_kernel,
        out_shape=(jax.ShapeDtypeStruct((1, positions, WIDTH), jnp.bfloat16),) * count,
        grid=(2,),
        in_specs=[pl.BlockSpec((step,) + x.shape[1:], lambda i: (i, 0, 0, 0))],
        out_specs=(pl.BlockSpec((1, step, WIDTH), lambda i: (0, i, 0)),) * count,
        cost_estimate=pl.CostEstimate(flops=0, bytes_accessed=1_800_000, transcendentals=0),
    )(x)


def along(x, axis, shift):
    return lax.ppermute(x, axis, [(i, (i + shift) % 4) for i in range(4)])


def fetch_pairs():
    def spot(x, z, core, y):
        return (((x * 8 + z % 8) * 2 + core) * 2 + z // 8) * 4 + y

    pairs = []
    for x in range(4):
        for y in range(4):
            near = (4 * x + y) // 2
            for core, far in ((0, near - 3), (1, 4 - near)):
                for z in range(16):
                    pairs.append((spot(x, (z + far) % 16, core, y), spot(x, z, core, y)))
    return pairs


PART = 40


def assemble_kernel(at_ref, own_ref, other_ref, out_ref):
    x, y, z, core = [at_ref[n] for n in range(4)]
    rows = out_ref.shape[2]

    def copy(source, slot, mirrored):
        for n in range(8):
            near = lax.rem(n - z + 11, 8)
            first = 2 * jnp.where(mirrored, 7 - near, near)
            for half in range(2):
                owner = first + half
                s = lax.rem(x - lax.div(owner, 4) + 4, 4)
                t = lax.rem(y - lax.rem(owner, 4) + 4, 4)
                if half == 0:
                    out_ref[n, slot, :PART] = source[s, t]
                else:
                    out_ref[n, slot, PART:] = source[s, t, 2 * PART - rows :]

    copy(own_ref, 0, core == 1)
    copy(other_ref, 1, core == 0)


def assemble(at, own, other, rows):
    vmem = pl.BlockSpec(memory_space=pltpu.VMEM)
    return pl.pallas_call(
        assemble_kernel,
        out_shape=jax.ShapeDtypeStruct((8, 2, rows, WIDTH), jnp.bfloat16),
        in_specs=[pl.BlockSpec(memory_space=pltpu.SMEM), vmem, vmem],
        out_specs=vmem,
        compiler_params=pltpu.CompilerParams(vmem_limit_bytes=10 << 20),
        cost_estimate=pl.CostEstimate(flops=0, bytes_accessed=1000, transcendentals=0),
    )(at, own, other)


def gather_weight(shard, later):
    rows = shard.shape[0]
    y = lax.axis_index("y")
    held = jnp.where(y % 2 == 0, shard[:PART], shard[rows - PART :])
    held = lax.ppermute(held, AXES, fetch_pairs())
    held, later = lax.optimization_barrier((held, later))
    held = jnp.stack([held] + [along(held, "y", s) for s in (1, 2, 3)])
    held = jnp.stack([held] + [along(held, "clip", s) for s in (1, 2, 3)])
    other = lax.ppermute(held, "core", [(0, 1), (1, 0)])
    at = jnp.stack([lax.axis_index(n) for n in ("clip", "y", "zl", "core")]).astype(jnp.int32)
    pairs = assemble(at, held, other, rows)
    even = lax.axis_index("core") == 0
    pairs = jnp.where(even, pairs, pairs[:, ::-1])
    return pairs.reshape(WIDTH, WIDTH), later


def sum_of_terms(pieces):
    own = jnp.sum(pieces.astype(jnp.float32), axis=0)
    other = lax.ppermute(own, "core", [(0, 1), (1, 0)])
    core = lax.axis_index("core")
    low = jnp.where(core == 0, own, other)
    high = jnp.where(core == 0, other, own)
    return jnp.concatenate([low, high[1:]], axis=0).reshape(WIDTH)


def per_device(query_states, key_states, value_states, grad_output, branch_gate, out_weight):
    packed = pack((query_states, key_states, value_states, grad_output))
    weight, packed = gather_weight(out_weight, packed)
    moved = lax.all_to_all(packed, GROUP, split_axis=0, concat_axis=0, tiled=True)
    grads = attend(moved, weight, branch_gate.reshape(1, WIDTH))
    returned = lax.all_to_all(grads, GROUP, split_axis=0, concat_axis=0, tiled=True)
    sent = returned.reshape(returned.shape[0], ROWS_OUT, LANES)
    gate_grad = sum_of_terms(sent[:, 3 * TILES :])
    return tuple(unpack(returned, 3)) + (gate_grad,)


def solution(mesh):
    split = Mesh(mesh.devices.reshape(mesh.shape["clip"], 8, 2, 2, 4), AXES)
    rows = P(AXES, None, None)
    return jax.shard_map(
        per_device,
        mesh=split,
        in_specs=(rows, rows, rows, rows, P("clip"), P(("zl", "core"), None)),
        out_specs=(rows, rows, rows, P("clip")),
        check_vma=False,
    )
```

```python
import functools

import jax
import jax.numpy as jnp
from jax import lax
from jax.experimental import pallas as pl
from jax.experimental.pallas import tpu as pltpu
from jax.sharding import Mesh
from jax.sharding import PartitionSpec as P

HEADS = 16
HEAD_DIM = 72
LANES = 128
WIDTH = HEADS * HEAD_DIM
TILES = WIDTH // LANES
AXES = ("clip", "zl", "core", "zh", "y")
GROUP = ("zl", "core", "zh", "y")
GATE_ROWS = 5
ROWS_OUT = 3 * TILES + GATE_ROWS
FACTOR = HEAD_DIM ** (-0.5)


def head_tiles(head):
    first = head * HEAD_DIM // LANES
    last = (head * HEAD_DIM + HEAD_DIM - 1) // LANES
    return first, last + 1


def attend_kernel(moved_ref, w_ref, gate_ref, out_ref, x_ref, da_ref):
    f32, bf16 = jnp.float32, jnp.bfloat16
    nt = (((1,), (1,)), ((), ()))
    nn = (((1,), (0,)), ((), ()))
    tn = (((0,), (0,)), ((), ()))
    frames = moved_ref.shape[0]
    x_ref[...] = jnp.transpose(moved_ref[...].reshape(frames, 4 * TILES, LANES), (1, 0, 2))

    def cat(first, last):
        parts = [x_ref[t] for t in range(first, last)]
        return parts[0] if len(parts) == 1 else jnp.concatenate(parts, axis=1)

    go = cat(3 * TILES, 4 * TILES)
    gated = (go.astype(f32) * gate_ref[...]).astype(bf16)
    da_ref[...] = lax.dot_general(gated, w_ref[...], nt, preferred_element_type=f32).astype(bf16)

    acc = {}

    def add(kind, first, value):
        for n in range(2):
            key = (kind, first + n)
            part = value[:, n * LANES : (n + 1) * LANES]
            acc[key] = acc[key] + part if key in acc else part

    lane = lax.broadcasted_iota(jnp.int32, (frames, 2 * LANES), 1)

    def both_heads(value, start):
        zero = jnp.zeros_like(value)
        heads = [
            jnp.where((lane >= at) & (lane < at + HEAD_DIM), value, zero)
            for at in (start, start + HEAD_DIM)
        ]
        return jnp.concatenate(heads, axis=0)

    def operands(pair):
        tile, start = divmod(2 * pair * HEAD_DIM, LANES)
        q, k, v = [cat(n * TILES + tile, n * TILES + tile + 2) for n in range(3)]
        g = da_ref[:, tile * LANES : (tile + 2) * LANES]
        return (tile, q, g) + tuple(both_heads(value, start) for value in (q, k, v, g))

    def heads_of(value):
        return value[:, :frames], value[:, frames:]

    for first in range(0, HEADS // 2, 4):
        ops = [operands(pair) for pair in range(first, first + 4)]
        scores = [lax.dot_general(o[1], o[4], nt, preferred_element_type=f32) for o in ops]
        dprobs = [lax.dot_general(o[2], o[5], nt, preferred_element_type=f32) for o in ops]
        scores = [s * FACTOR for pair in scores for s in heads_of(pair)]
        dprobs = [d for pair in dprobs for d in heads_of(pair)]
        expon = [jnp.exp(s - jnp.max(s, axis=-1, keepdims=True)) for s in scores]
        probs = [e / jnp.sum(e, axis=-1, keepdims=True) for e in expon]
        delta = [jnp.sum(p * d, axis=-1, keepdims=True) for p, d in zip(probs, dprobs)]
        dscores = [
            (p * (d - e) * FACTOR).astype(bf16) for p, d, e in zip(probs, dprobs, delta)
        ]
        probs = [p.astype(bf16) for p in probs]
        for n, (tile, _, _, q, k, v, g) in enumerate(ops):
            p, d = probs[2 * n : 2 * n + 2], dscores[2 * n : 2 * n + 2]
            p_wide, d_wide = jnp.concatenate(p, axis=1), jnp.concatenate(d, axis=1)
            p_tall, d_tall = jnp.concatenate(p, axis=0), jnp.concatenate(d, axis=0)
            add("o", tile, lax.dot_general(p_wide, v, nn, preferred_element_type=f32))
            add("v", tile, lax.dot_general(p_tall, g, tn, preferred_element_type=f32))
            add("q", tile, lax.dot_general(d_wide, k, nn, preferred_element_type=f32))
            add("k", tile, lax.dot_general(d_tall, q, tn, preferred_element_type=f32))
    attn = jnp.concatenate([acc[("o", t)].astype(bf16) for t in range(TILES)], axis=1)
    branch = lax.dot_general(attn, w_ref[...], nn, preferred_element_type=f32)
    terms = jnp.sum(go.astype(f32) * branch, axis=0, keepdims=True)
    rows = [terms[:, t * LANES : (t + 1) * LANES] for t in range(TILES)]

    out = [acc[(kind, t)].astype(bf16) for kind in "qkv" for t in range(TILES)]
    for n in range(GATE_ROWS):
        pair = [jnp.broadcast_to(rows[m], (8, LANES)) for m in (n, n + GATE_ROWS - 1)]
        block = jnp.concatenate(pair, axis=0).astype(bf16)
        out.append(jnp.concatenate([block] * (frames // 16), axis=0))
    out_ref[...] = jnp.transpose(jnp.stack(out), (1, 0, 2)).reshape(out_ref.shape)


def attend(x, weight, gate):
    frames = x.shape[0]
    vmem = pl.BlockSpec(memory_space=pltpu.VMEM)
    return pl.pallas_call(
        attend_kernel,
        out_shape=jax.ShapeDtypeStruct((frames, ROWS_OUT // 4, 4, LANES), jnp.bfloat16),
        in_specs=[vmem, vmem, vmem],
        out_specs=vmem,
        scratch_shapes=[
            pltpu.VMEM((4 * TILES, frames, LANES), jnp.bfloat16),
            pltpu.VMEM((frames, WIDTH), jnp.bfloat16),
        ],
        compiler_params=pltpu.CompilerParams(vmem_limit_bytes=12 << 20),
        cost_estimate=pl.CostEstimate(
            flops=1_500_000_000, bytes_accessed=5_000_000, transcendentals=300_000
        ),
    )(x, weight, gate)


def pack_kernel(*refs):
    out_ref = refs[-1]
    tiles = [ref[0, :, t * LANES : (t + 1) * LANES] for ref in refs[:-1] for t in range(TILES)]
    out_ref[...] = jnp.transpose(jnp.stack(tiles), (1, 0, 2)).reshape(out_ref.shape)


def pack(arrays):
    positions = arrays[0].shape[1]
    step = positions // 2
    shape = (positions, len(arrays) * TILES // 4, 4, LANES)
    return pl.pallas_call(
        pack_kernel,
        out_shape=jax.ShapeDtypeStruct(shape, jnp.bfloat16),
        grid=(2,),
        in_specs=[pl.BlockSpec((1, step, WIDTH), lambda i: (0, i, 0))] * len(arrays),
        out_specs=pl.BlockSpec((step,) + shape[1:], lambda i: (i, 0, 0, 0)),
        cost_estimate=pl.CostEstimate(flops=0, bytes_accessed=2_400_000, transcendentals=0),
    )(*arrays)


def unpack_kernel(x_ref, *out_refs):
    positions, quads = x_ref.shape[0], x_ref.shape[1]
    tiles = jnp.transpose(x_ref[...].reshape(positions, quads * 4, LANES), (1, 0, 2))
    for n, ref in enumerate(out_refs):
        for t in range(TILES):
            ref[0, :, t * LANES : (t + 1) * LANES] = tiles[n * TILES + t]


def unpack(x, count):
    positions = x.shape[0]
    step = positions // 2
    return pl.pallas_call(
        unpack_kernel,
        out_shape=(jax.ShapeDtypeStruct((1, positions, WIDTH), jnp.bfloat16),) * count,
        grid=(2,),
        in_specs=[pl.BlockSpec((step,) + x.shape[1:], lambda i: (i, 0, 0, 0))],
        out_specs=(pl.BlockSpec((1, step, WIDTH), lambda i: (0, i, 0)),) * count,
        cost_estimate=pl.CostEstimate(flops=0, bytes_accessed=1_800_000, transcendentals=0),
    )(x)


def along(x, axis, shift):
    return lax.ppermute(x, axis, [(i, (i + shift) % 4) for i in range(4)])


def fetch_pairs():
    def spot(x, z, core, y):
        return (((x * 8 + z % 8) * 2 + core) * 2 + z // 8) * 4 + y

    pairs = []
    for x in range(4):
        for y in range(4):
            near = (4 * x + y) // 2
            for core, far in ((0, near - 3), (1, 4 - near)):
                for z in range(16):
                    pairs.append((spot(x, (z + far) % 16, core, y), spot(x, z, core, y)))
    return pairs


PART = 40


def same(x, passes):
    for n in range(passes):
        one = jnp.where(lax.axis_index("clip") >= -n, 1.0, 2.0).astype(x.dtype)
        x = lax.optimization_barrier(x * one)
    return x


def assemble_kernel(at_ref, own_ref, other_ref, out_ref):
    x, y, z, core = [at_ref[n] for n in range(4)]
    rows = out_ref.shape[2]

    def copy(source, slot, mirrored):
        for n in range(8):
            near = lax.rem(n - z + 11, 8)
            first = 2 * jnp.where(mirrored, 7 - near, near)
            for half in range(2):
                owner = first + half
                s = lax.rem(x - lax.div(owner, 4) + 4, 4)
                t = lax.rem(y - lax.rem(owner, 4) + 4, 4)
                if half == 0:
                    out_ref[n, slot, :PART] = source[s, t]
                else:
                    out_ref[n, slot, PART:] = source[s, t, 2 * PART - rows :]

    copy(own_ref, 0, core == 1)
    copy(other_ref, 1, core == 0)


def assemble(at, own, other, rows):
    vmem = pl.BlockSpec(memory_space=pltpu.VMEM)
    return pl.pallas_call(
        assemble_kernel,
        out_shape=jax.ShapeDtypeStruct((8, 2, rows, WIDTH), jnp.bfloat16),
        in_specs=[pl.BlockSpec(memory_space=pltpu.SMEM), vmem, vmem],
        out_specs=vmem,
        compiler_params=pltpu.CompilerParams(vmem_limit_bytes=10 << 20),
        cost_estimate=pl.CostEstimate(flops=0, bytes_accessed=1000, transcendentals=0),
    )(at, own, other)


def gather_weight(shard, later):
    rows = shard.shape[0]
    y = lax.axis_index("y")
    held = jnp.where(y % 2 == 0, shard[:PART], shard[rows - PART :])
    held = lax.ppermute(held, AXES, fetch_pairs())
    held, _ = lax.optimization_barrier((held, later))
    held = same(held, 2)
    held = jnp.stack([held] + [along(held, "y", s) for s in (1, 2, 3)])
    held = jnp.stack([held] + [along(held, "clip", s) for s in (1, 2, 3)])
    other = lax.ppermute(held, "core", [(0, 1), (1, 0)])
    at = jnp.stack([lax.axis_index(n) for n in ("clip", "y", "zl", "core")]).astype(jnp.int32)
    pairs = assemble(at, held, other, rows)
    even = lax.axis_index("core") == 0
    pairs = same(jnp.where(even, pairs, pairs[:, ::-1]), 2)
    return pairs.reshape(WIDTH, WIDTH)


def sum_of_terms(pieces):
    own = jnp.sum(pieces.astype(jnp.float32), axis=0)
    other = lax.ppermute(own, "core", [(0, 1), (1, 0)])
    core = lax.axis_index("core")
    low = jnp.where(core == 0, own, other)
    high = jnp.where(core == 0, other, own)
    return jnp.concatenate([low, high[1:]], axis=0).reshape(WIDTH)


def per_device(query_states, key_states, value_states, grad_output, branch_gate, out_weight):
    packed = pack((query_states, key_states, value_states, grad_output))
    weight = gather_weight(out_weight, packed)
    moved = lax.all_to_all(packed, GROUP, split_axis=0, concat_axis=0, tiled=True)
    grads = attend(moved, weight, branch_gate.reshape(1, WIDTH))
    returned = lax.all_to_all(grads, GROUP, split_axis=0, concat_axis=0, tiled=True)
    sent = returned.reshape(returned.shape[0], ROWS_OUT, LANES)
    gate_grad = sum_of_terms(sent[:, 3 * TILES :])
    return tuple(unpack(returned, 3)) + (gate_grad,)


def solution(mesh):
    split = Mesh(mesh.devices.reshape(mesh.shape["clip"], 8, 2, 2, 4), AXES)
    rows = P(AXES, None, None)
    return jax.shard_map(
        per_device,
        mesh=split,
        in_specs=(rows, rows, rows, rows, P("clip"), P(("zl", "core"), None)),
        out_specs=(rows, rows, rows, P("clip")),
        check_vma=False,
    )
```

```python
import functools

import jax
import jax.numpy as jnp
from jax import lax
from jax.experimental import pallas as pl
from jax.experimental.pallas import tpu as pltpu
from jax.sharding import Mesh
from jax.sharding import PartitionSpec as P

HEADS = 16
HEAD_DIM = 72
LANES = 128
WIDTH = HEADS * HEAD_DIM
TILES = WIDTH // LANES
AXES = ("clip", "zl", "core", "zh", "y")
GROUP = ("zl", "core", "zh", "y")
GATE_ROWS = 5
ROWS_OUT = 3 * TILES + GATE_ROWS
FACTOR = HEAD_DIM ** (-0.5)


def head_tiles(head):
    first = head * HEAD_DIM // LANES
    last = (head * HEAD_DIM + HEAD_DIM - 1) // LANES
    return first, last + 1


def attend_kernel(moved_ref, w_ref, gate_ref, out_ref, x_ref, da_ref):
    f32, bf16 = jnp.float32, jnp.bfloat16
    nt = (((1,), (1,)), ((), ()))
    nn = (((1,), (0,)), ((), ()))
    tn = (((0,), (0,)), ((), ()))
    frames = moved_ref.shape[0]
    x_ref[...] = jnp.transpose(moved_ref[...].reshape(frames, 4 * TILES, LANES), (1, 0, 2))

    def cat(first, last):
        parts = [x_ref[t] for t in range(first, last)]
        return parts[0] if len(parts) == 1 else jnp.concatenate(parts, axis=1)

    go = cat(3 * TILES, 4 * TILES)
    gated = (go.astype(f32) * gate_ref[...]).astype(bf16)
    da_ref[...] = lax.dot_general(gated, w_ref[...], nt, preferred_element_type=f32).astype(bf16)

    acc = {}

    def add(kind, first, value):
        for n in range(2):
            key = (kind, first + n)
            part = value[:, n * LANES : (n + 1) * LANES]
            acc[key] = acc[key] + part if key in acc else part

    lane = lax.broadcasted_iota(jnp.int32, (frames, 2 * LANES), 1)

    def both_heads(value, start):
        zero = jnp.zeros_like(value)
        heads = [
            jnp.where((lane >= at) & (lane < at + HEAD_DIM), value, zero)
            for at in (start, start + HEAD_DIM)
        ]
        return jnp.concatenate(heads, axis=0)

    def operands(pair):
        tile, start = divmod(2 * pair * HEAD_DIM, LANES)
        q, k, v = [cat(n * TILES + tile, n * TILES + tile + 2) for n in range(3)]
        g = da_ref[:, tile * LANES : (tile + 2) * LANES]
        return (tile, q, g) + tuple(both_heads(value, start) for value in (q, k, v, g))

    def heads_of(value):
        return value[:, :frames], value[:, frames:]

    for first in range(0, HEADS // 2, 4):
        ops = [operands(pair) for pair in range(first, first + 4)]
        scores = [lax.dot_general(o[1], o[4], nt, preferred_element_type=f32) for o in ops]
        dprobs = [lax.dot_general(o[2], o[5], nt, preferred_element_type=f32) for o in ops]
        scores = [s * FACTOR for pair in scores for s in heads_of(pair)]
        dprobs = [d for pair in dprobs for d in heads_of(pair)]
        expon = [jnp.exp(s - jnp.max(s, axis=-1, keepdims=True)) for s in scores]
        probs = [e / jnp.sum(e, axis=-1, keepdims=True) for e in expon]
        delta = [jnp.sum(p * d, axis=-1, keepdims=True) for p, d in zip(probs, dprobs)]
        dscores = [
            (p * (d - e) * FACTOR).astype(bf16) for p, d, e in zip(probs, dprobs, delta)
        ]
        probs = [p.astype(bf16) for p in probs]
        for n, (tile, _, _, q, k, v, g) in enumerate(ops):
            p, d = probs[2 * n : 2 * n + 2], dscores[2 * n : 2 * n + 2]
            p_wide, d_wide = jnp.concatenate(p, axis=1), jnp.concatenate(d, axis=1)
            p_tall, d_tall = jnp.concatenate(p, axis=0), jnp.concatenate(d, axis=0)
            add("o", tile, lax.dot_general(p_wide, v, nn, preferred_element_type=f32))
            add("v", tile, lax.dot_general(p_tall, g, tn, preferred_element_type=f32))
            add("q", tile, lax.dot_general(d_wide, k, nn, preferred_element_type=f32))
            add("k", tile, lax.dot_general(d_tall, q, tn, preferred_element_type=f32))
    attn = jnp.concatenate([acc[("o", t)].astype(bf16) for t in range(TILES)], axis=1)
    branch = lax.dot_general(attn, w_ref[...], nn, preferred_element_type=f32)
    terms = jnp.sum(go.astype(f32) * branch, axis=0, keepdims=True)
    rows = [terms[:, t * LANES : (t + 1) * LANES] for t in range(TILES)]

    out = [acc[(kind, t)].astype(bf16) for kind in "qkv" for t in range(TILES)]
    for n in range(GATE_ROWS):
        pair = [jnp.broadcast_to(rows[m], (8, LANES)) for m in (n, n + GATE_ROWS - 1)]
        block = jnp.concatenate(pair, axis=0).astype(bf16)
        out.append(jnp.concatenate([block] * (frames // 16), axis=0))
    out_ref[...] = jnp.transpose(jnp.stack(out), (1, 0, 2)).reshape(out_ref.shape)


def attend(x, weight, gate):
    frames = x.shape[0]
    vmem = pl.BlockSpec(memory_space=pltpu.VMEM)
    return pl.pallas_call(
        attend_kernel,
        out_shape=jax.ShapeDtypeStruct((frames, ROWS_OUT // 4, 4, LANES), jnp.bfloat16),
        in_specs=[vmem, vmem, vmem],
        out_specs=vmem,
        scratch_shapes=[
            pltpu.VMEM((4 * TILES, frames, LANES), jnp.bfloat16),
            pltpu.VMEM((frames, WIDTH), jnp.bfloat16),
        ],
        compiler_params=pltpu.CompilerParams(vmem_limit_bytes=12 << 20),
        cost_estimate=pl.CostEstimate(
            flops=1_500_000_000, bytes_accessed=5_000_000, transcendentals=300_000
        ),
    )(x, weight, gate)


def pack_kernel(*refs):
    out_ref = refs[-1]
    tiles = [ref[0, :, t * LANES : (t + 1) * LANES] for ref in refs[:-1] for t in range(TILES)]
    out_ref[...] = jnp.transpose(jnp.stack(tiles), (1, 0, 2)).reshape(out_ref.shape)


def pack(arrays):
    positions = arrays[0].shape[1]
    step = positions // 2
    shape = (positions, len(arrays) * TILES // 4, 4, LANES)
    return pl.pallas_call(
        pack_kernel,
        out_shape=jax.ShapeDtypeStruct(shape, jnp.bfloat16),
        grid=(2,),
        in_specs=[pl.BlockSpec((1, step, WIDTH), lambda i: (0, i, 0))] * len(arrays),
        out_specs=pl.BlockSpec((step,) + shape[1:], lambda i: (i, 0, 0, 0)),
        cost_estimate=pl.CostEstimate(flops=0, bytes_accessed=2_400_000, transcendentals=0),
    )(*arrays)


def unpack_kernel(x_ref, *out_refs):
    positions, quads = x_ref.shape[0], x_ref.shape[1]
    tiles = jnp.transpose(x_ref[...].reshape(positions, quads * 4, LANES), (1, 0, 2))
    for n, ref in enumerate(out_refs):
        for t in range(TILES):
            ref[0, :, t * LANES : (t + 1) * LANES] = tiles[n * TILES + t]


def unpack(x, count):
    positions = x.shape[0]
    step = positions // 2
    return pl.pallas_call(
        unpack_kernel,
        out_shape=(jax.ShapeDtypeStruct((1, positions, WIDTH), jnp.bfloat16),) * count,
        grid=(2,),
        in_specs=[pl.BlockSpec((step,) + x.shape[1:], lambda i: (i, 0, 0, 0))],
        out_specs=(pl.BlockSpec((1, step, WIDTH), lambda i: (0, i, 0)),) * count,
        cost_estimate=pl.CostEstimate(flops=0, bytes_accessed=1_800_000, transcendentals=0),
    )(x)


def along(x, axis, shift):
    return lax.ppermute(x, axis, [(i, (i + shift) % 4) for i in range(4)])


def fetch_pairs():
    def spot(x, z, core, y):
        return (((x * 8 + z % 8) * 2 + core) * 2 + z // 8) * 4 + y

    pairs = []
    for x in range(4):
        for y in range(4):
            near = (4 * x + y) // 2
            for core, far in ((0, near - 3), (1, 4 - near)):
                for z in range(16):
                    pairs.append((spot(x, (z + far) % 16, core, y), spot(x, z, core, y)))
    return pairs


PART = 40


def same(x, passes):
    for n in range(passes):
        one = jnp.where(lax.axis_index("clip") >= -n, 1.0, 2.0).astype(x.dtype)
        x = lax.optimization_barrier(x * one)
    return x


def assemble_kernel(at_ref, own_ref, other_ref, out_ref):
    x, y, z, core = [at_ref[n] for n in range(4)]
    rows = out_ref.shape[2]

    def copy(source, slot, mirrored):
        for n in range(8):
            near = lax.rem(n - z + 11, 8)
            first = 2 * jnp.where(mirrored, 7 - near, near)
            for half in range(2):
                owner = first + half
                s = lax.rem(x - lax.div(owner, 4) + 4, 4)
                t = lax.rem(y - lax.rem(owner, 4) + 4, 4)
                if half == 0:
                    out_ref[n, slot, :PART] = source[s, t]
                else:
                    out_ref[n, slot, PART:] = source[s, t, 2 * PART - rows :]

    copy(own_ref, 0, core == 1)
    copy(other_ref, 1, core == 0)


def assemble(at, own, other, rows):
    vmem = pl.BlockSpec(memory_space=pltpu.VMEM)
    return pl.pallas_call(
        assemble_kernel,
        out_shape=jax.ShapeDtypeStruct((8, 2, rows, WIDTH), jnp.bfloat16),
        in_specs=[pl.BlockSpec(memory_space=pltpu.SMEM), vmem, vmem],
        out_specs=vmem,
        compiler_params=pltpu.CompilerParams(vmem_limit_bytes=10 << 20),
        cost_estimate=pl.CostEstimate(flops=0, bytes_accessed=1000, transcendentals=0),
    )(at, own, other)


def gather_weight(shard, later):
    rows = shard.shape[0]
    y = lax.axis_index("y")
    held = lax.ppermute(shard, AXES, fetch_pairs())
    held, _ = lax.optimization_barrier((held, later))
    held = jnp.where(y % 2 == 0, held[:PART], held[rows - PART :])
    held = same(held, 2)
    held = jnp.stack([held] + [along(held, "y", s) for s in (1, 2, 3)])
    held = jnp.stack([held] + [along(held, "clip", s) for s in (1, 2, 3)])
    other = lax.ppermute(held, "core", [(0, 1), (1, 0)])
    at = jnp.stack([lax.axis_index(n) for n in ("clip", "y", "zl", "core")]).astype(jnp.int32)
    pairs = assemble(at, held, other, rows)
    even = lax.axis_index("core") == 0
    pairs = same(jnp.where(even, pairs, pairs[:, ::-1]), 2)
    return pairs.reshape(WIDTH, WIDTH)


def sum_of_terms(pieces):
    own = jnp.sum(pieces.astype(jnp.float32), axis=0)
    other = lax.ppermute(own, "core", [(0, 1), (1, 0)])
    core = lax.axis_index("core")
    low = jnp.where(core == 0, own, other)
    high = jnp.where(core == 0, other, own)
    return jnp.concatenate([low, high[1:]], axis=0).reshape(WIDTH)


def per_device(query_states, key_states, value_states, grad_output, branch_gate, out_weight):
    packed = pack((query_states, key_states, value_states, grad_output))
    weight = gather_weight(out_weight, packed)
    moved = lax.all_to_all(packed, GROUP, split_axis=0, concat_axis=0, tiled=True)
    grads = attend(moved, weight, branch_gate.reshape(1, WIDTH))
    returned = lax.all_to_all(grads, GROUP, split_axis=0, concat_axis=0, tiled=True)
    sent = returned.reshape(returned.shape[0], ROWS_OUT, LANES)
    gate_grad = sum_of_terms(sent[:, 3 * TILES :])
    return tuple(unpack(returned, 3)) + (gate_grad,)


def solution(mesh):
    split = Mesh(mesh.devices.reshape(mesh.shape["clip"], 8, 2, 2, 4), AXES)
    rows = P(AXES, None, None)
    return jax.shard_map(
        per_device,
        mesh=split,
        in_specs=(rows, rows, rows, rows, P("clip"), P(("zl", "core"), None)),
        out_specs=(rows, rows, rows, P("clip")),
        check_vma=False,
    )
```

```python
import functools

import jax
import jax.numpy as jnp
from jax import lax
from jax.experimental import pallas as pl
from jax.experimental.pallas import tpu as pltpu
from jax.sharding import Mesh
from jax.sharding import PartitionSpec as P

HEADS = 16
HEAD_DIM = 72
LANES = 128
WIDTH = HEADS * HEAD_DIM
TILES = WIDTH // LANES
AXES = ("clip", "zl", "core", "zh", "y")
GROUP = ("zl", "core", "zh", "y")
CHUNKS = 4
GATE_ROWS = 5
ROWS_OUT = 3 * TILES + GATE_ROWS
FACTOR = HEAD_DIM ** (-0.5)


def head_tiles(head):
    first = head * HEAD_DIM // LANES
    last = (head * HEAD_DIM + HEAD_DIM - 1) // LANES
    return first, last + 1


def attend_kernel(moved_hbm, w_ref, gate_ref, out_ref, moved_ref, x_ref, da_ref, sems):
    f32, bf16 = jnp.float32, jnp.bfloat16
    nt = (((1,), (1,)), ((), ()))
    nn = (((1,), (0,)), ((), ()))
    tn = (((0,), (0,)), ((), ()))
    frames = moved_ref.shape[0]
    step = frames // CHUNKS
    spans = [pl.ds(n * step, step) for n in range(CHUNKS)]
    loads = [
        pltpu.make_async_copy(moved_hbm.at[span], moved_ref.at[span], sems.at[n])
        for n, span in enumerate(spans)
    ]
    for load in loads:
        load.start()
    for load, span in zip(loads, spans):
        load.wait()
        part = moved_ref[span].reshape(step, 4 * TILES, LANES)
        x_ref[:, span] = jnp.transpose(part, (1, 0, 2))

    def cat(first, last):
        parts = [x_ref[t] for t in range(first, last)]
        return parts[0] if len(parts) == 1 else jnp.concatenate(parts, axis=1)

    go = cat(3 * TILES, 4 * TILES)
    gated = (go.astype(f32) * gate_ref[...]).astype(bf16)
    da_ref[...] = lax.dot_general(gated, w_ref[...], nt, preferred_element_type=f32).astype(bf16)

    acc = {}

    def add(kind, first, value):
        for n in range(2):
            key = (kind, first + n)
            part = value[:, n * LANES : (n + 1) * LANES]
            acc[key] = acc[key] + part if key in acc else part

    lane = lax.broadcasted_iota(jnp.int32, (frames, 2 * LANES), 1)

    def both_heads(value, start):
        zero = jnp.zeros_like(value)
        heads = [
            jnp.where((lane >= at) & (lane < at + HEAD_DIM), value, zero)
            for at in (start, start + HEAD_DIM)
        ]
        return jnp.concatenate(heads, axis=0)

    def operands(pair):
        tile, start = divmod(2 * pair * HEAD_DIM, LANES)
        q, k, v = [cat(n * TILES + tile, n * TILES + tile + 2) for n in range(3)]
        g = da_ref[:, tile * LANES : (tile + 2) * LANES]
        return (tile, q, g) + tuple(both_heads(value, start) for value in (q, k, v, g))

    def heads_of(value):
        return value[:, :frames], value[:, frames:]

    for first in range(0, HEADS // 2, 4):
        ops = [operands(pair) for pair in range(first, first + 4)]
        scores = [lax.dot_general(o[1], o[4], nt, preferred_element_type=f32) for o in ops]
        dprobs = [lax.dot_general(o[2], o[5], nt, preferred_element_type=f32) for o in ops]
        scores = [s * FACTOR for pair in scores for s in heads_of(pair)]
        dprobs = [d for pair in dprobs for d in heads_of(pair)]
        expon = [jnp.exp(s - jnp.max(s, axis=-1, keepdims=True)) for s in scores]
        probs = [e / jnp.sum(e, axis=-1, keepdims=True) for e in expon]
        delta = [jnp.sum(p * d, axis=-1, keepdims=True) for p, d in zip(probs, dprobs)]
        dscores = [
            (p * (d - e) * FACTOR).astype(bf16) for p, d, e in zip(probs, dprobs, delta)
        ]
        probs = [p.astype(bf16) for p in probs]
        for n, (tile, _, _, q, k, v, g) in enumerate(ops):
            p, d = probs[2 * n : 2 * n + 2], dscores[2 * n : 2 * n + 2]
            p_wide, d_wide = jnp.concatenate(p, axis=1), jnp.concatenate(d, axis=1)
            p_tall, d_tall = jnp.concatenate(p, axis=0), jnp.concatenate(d, axis=0)
            add("o", tile, lax.dot_general(p_wide, v, nn, preferred_element_type=f32))
            add("v", tile, lax.dot_general(p_tall, g, tn, preferred_element_type=f32))
            add("q", tile, lax.dot_general(d_wide, k, nn, preferred_element_type=f32))
            add("k", tile, lax.dot_general(d_tall, q, tn, preferred_element_type=f32))
    attn = jnp.concatenate([acc[("o", t)].astype(bf16) for t in range(TILES)], axis=1)
    branch = lax.dot_general(attn, w_ref[...], nn, preferred_element_type=f32)
    terms = jnp.sum(go.astype(f32) * branch, axis=0, keepdims=True)
    rows = [terms[:, t * LANES : (t + 1) * LANES] for t in range(TILES)]

    out = [acc[(kind, t)].astype(bf16) for kind in "qkv" for t in range(TILES)]
    for n in range(GATE_ROWS):
        pair = [jnp.broadcast_to(rows[m], (8, LANES)) for m in (n, n + GATE_ROWS - 1)]
        block = jnp.concatenate(pair, axis=0).astype(bf16)
        out.append(jnp.concatenate([block] * (frames // 16), axis=0))
    out_ref[...] = jnp.transpose(jnp.stack(out), (1, 0, 2)).reshape(out_ref.shape)


def attend(x, weight, gate):
    frames = x.shape[0]
    vmem = pl.BlockSpec(memory_space=pltpu.VMEM)
    return pl.pallas_call(
        attend_kernel,
        out_shape=jax.ShapeDtypeStruct((frames, ROWS_OUT // 4, 4, LANES), jnp.bfloat16),
        in_specs=[pl.BlockSpec(memory_space=pl.ANY), vmem, vmem],
        out_specs=vmem,
        scratch_shapes=[
            pltpu.VMEM(x.shape, jnp.bfloat16),
            pltpu.VMEM((4 * TILES, frames, LANES), jnp.bfloat16),
            pltpu.VMEM((frames, WIDTH), jnp.bfloat16),
            pltpu.SemaphoreType.DMA((CHUNKS,)),
        ],
        compiler_params=pltpu.CompilerParams(vmem_limit_bytes=16 << 20),
        cost_estimate=pl.CostEstimate(
            flops=1_500_000_000, bytes_accessed=5_000_000, transcendentals=300_000
        ),
    )(x, weight, gate)


def pack_kernel(*refs):
    out_ref = refs[-1]
    tiles = [ref[0, :, t * LANES : (t + 1) * LANES] for ref in refs[:-1] for t in range(TILES)]
    out_ref[...] = jnp.transpose(jnp.stack(tiles), (1, 0, 2)).reshape(out_ref.shape)


def pack(arrays):
    positions = arrays[0].shape[1]
    step = positions // 2
    shape = (positions, len(arrays) * TILES // 4, 4, LANES)
    return pl.pallas_call(
        pack_kernel,
        out_shape=jax.ShapeDtypeStruct(shape, jnp.bfloat16),
        grid=(2,),
        in_specs=[pl.BlockSpec((1, step, WIDTH), lambda i: (0, i, 0))] * len(arrays),
        out_specs=pl.BlockSpec((step,) + shape[1:], lambda i: (i, 0, 0, 0)),
        cost_estimate=pl.CostEstimate(flops=0, bytes_accessed=2_400_000, transcendentals=0),
    )(*arrays)


def unpack_kernel(x_ref, *out_refs):
    positions, quads = x_ref.shape[0], x_ref.shape[1]
    tiles = jnp.transpose(x_ref[...].reshape(positions, quads * 4, LANES), (1, 0, 2))
    for n, ref in enumerate(out_refs):
        for t in range(TILES):
            ref[0, :, t * LANES : (t + 1) * LANES] = tiles[n * TILES + t]


def unpack(x, count):
    positions = x.shape[0]
    step = positions // 2
    return pl.pallas_call(
        unpack_kernel,
        out_shape=(jax.ShapeDtypeStruct((1, positions, WIDTH), jnp.bfloat16),) * count,
        grid=(2,),
        in_specs=[pl.BlockSpec((step,) + x.shape[1:], lambda i: (i, 0, 0, 0))],
        out_specs=(pl.BlockSpec((1, step, WIDTH), lambda i: (0, i, 0)),) * count,
        cost_estimate=pl.CostEstimate(flops=0, bytes_accessed=1_800_000, transcendentals=0),
    )(x)


def along(x, axis, shift):
    return lax.ppermute(x, axis, [(i, (i + shift) % 4) for i in range(4)])


def fetch_pairs():
    def spot(x, z, core, y):
        return (((x * 8 + z % 8) * 2 + core) * 2 + z // 8) * 4 + y

    pairs = []
    for x in range(4):
        for y in range(4):
            near = (4 * x + y) // 2
            for core, far in ((0, near - 3), (1, 4 - near)):
                for z in range(16):
                    pairs.append((spot(x, (z + far) % 16, core, y), spot(x, z, core, y)))
    return pairs


PART = 40


def same(x, passes):
    for n in range(passes):
        one = jnp.where(lax.axis_index("clip") >= -n, 1.0, 2.0).astype(x.dtype)
        x = lax.optimization_barrier(x * one)
    return x


def assemble_kernel(at_ref, own_ref, other_ref, out_ref):
    x, y, z, core = [at_ref[n] for n in range(4)]
    rows = out_ref.shape[2]

    def copy(source, slot, mirrored):
        for n in range(8):
            near = lax.rem(n - z + 11, 8)
            first = 2 * jnp.where(mirrored, 7 - near, near)
            for half in range(2):
                owner = first + half
                s = lax.rem(x - lax.div(owner, 4) + 4, 4)
                t = lax.rem(y - lax.rem(owner, 4) + 4, 4)
                if half == 0:
                    out_ref[n, slot, :PART] = source[s, t]
                else:
                    out_ref[n, slot, PART:] = source[s, t, 2 * PART - rows :]

    copy(own_ref, 0, core == 1)
    copy(other_ref, 1, core == 0)


def assemble(at, own, other, rows):
    vmem = pl.BlockSpec(memory_space=pltpu.VMEM)
    return pl.pallas_call(
        assemble_kernel,
        out_shape=jax.ShapeDtypeStruct((8, 2, rows, WIDTH), jnp.bfloat16),
        in_specs=[pl.BlockSpec(memory_space=pltpu.SMEM), vmem, vmem],
        out_specs=vmem,
        compiler_params=pltpu.CompilerParams(vmem_limit_bytes=10 << 20),
        cost_estimate=pl.CostEstimate(flops=0, bytes_accessed=1000, transcendentals=0),
    )(at, own, other)


def gather_weight(shard, later):
    rows = shard.shape[0]
    y = lax.axis_index("y")
    held = lax.ppermute(shard, AXES, fetch_pairs())
    held, _ = lax.optimization_barrier((held, later))
    held = jnp.where(y % 2 == 0, held[:PART], held[rows - PART :])
    held = same(held, 2)
    held = jnp.stack([held] + [along(held, "y", s) for s in (1, 2, 3)])
    held = jnp.stack([held] + [along(held, "clip", s) for s in (1, 2, 3)])
    other = lax.ppermute(held, "core", [(0, 1), (1, 0)])
    at = jnp.stack([lax.axis_index(n) for n in ("clip", "y", "zl", "core")]).astype(jnp.int32)
    pairs = assemble(at, held, other, rows)
    even = lax.axis_index("core") == 0
    pairs = same(jnp.where(even, pairs, pairs[:, ::-1]), 2)
    return pairs.reshape(WIDTH, WIDTH)


def sum_of_terms(pieces):
    own = jnp.sum(pieces.astype(jnp.float32), axis=0)
    other = lax.ppermute(own, "core", [(0, 1), (1, 0)])
    core = lax.axis_index("core")
    low = jnp.where(core == 0, own, other)
    high = jnp.where(core == 0, other, own)
    return jnp.concatenate([low, high[1:]], axis=0).reshape(WIDTH)


def per_device(query_states, key_states, value_states, grad_output, branch_gate, out_weight):
    packed = pack((query_states, key_states, value_states, grad_output))
    weight = gather_weight(out_weight, packed)
    moved = lax.all_to_all(packed, GROUP, split_axis=0, concat_axis=0, tiled=True)
    grads = attend(moved, weight, branch_gate.reshape(1, WIDTH))
    returned = lax.all_to_all(grads, GROUP, split_axis=0, concat_axis=0, tiled=True)
    sent = returned.reshape(returned.shape[0], ROWS_OUT, LANES)
    gate_grad = sum_of_terms(sent[:, 3 * TILES :])
    return tuple(unpack(returned, 3)) + (gate_grad,)


def solution(mesh):
    split = Mesh(mesh.devices.reshape(mesh.shape["clip"], 8, 2, 2, 4), AXES)
    rows = P(AXES, None, None)
    return jax.shard_map(
        per_device,
        mesh=split,
        in_specs=(rows, rows, rows, rows, P("clip"), P(("zl", "core"), None)),
        out_specs=(rows, rows, rows, P("clip")),
        check_vma=False,
    )
```
